32 devices in a mesh: groups: 2 (over y), wide: 4 (over z), lev: 2 (over x), fld: 2 (over core).
Axes of the slice: x: 2, y: 2, z: 4, core: 2. Of those that a mesh axis runs over, the one named last changes fastest.
Arguments:
- grid_state: bfloat16 [4, 3, 8, 512, 1024], P(('groups', 'fld'), None, 'lev', 'wide'), parts along dimension 0, may hold values from -6 to 6
- wave_slots: int32 [512], replicated, may hold values from 0 to 511, each once
- lat_basis: bfloat16 [512, 512, 512], P(('wide', 'lev')), may hold values from -0.25 to 0.25
- vert_modes: float32 [8, 8], replicated, may hold values from -1 to 1, as said below
- vert_rates: float32 [3, 8], replicated, may hold values from 0.05 to 20
- band_sizes: int32 [16], replicated, may hold values from 1 to 64, 512 in all
- norm_gain: float32 [24], replicated, may hold values from 0.25 to 1.75
- w_in: bfloat16 [512, 24], replicated, may hold values from -1.25 to 1.25
- band_bias: float32 [512, 16], replicated, may hold values from -6 to 6
- w_mid: bfloat16 [512, 512], replicated, may hold values from -0.25 to 0.25
- w_out: bfloat16 [24, 512], replicated, may hold values from -0.25 to 0.25
Outputs:
- spectral: float32 [512, 4, 3, 8, 2, 512], P(('wide', 'lev'), ('groups', 'fld')), parts along dimension 1
- new_state: bfloat16 [4, 3, 8, 512, 1024], P(('groups', 'fld'), None, None, ('wide', 'lev')), parts along dimension 0
The draws below stay inside these ranges and needn't reach their ends.
There are 2 independent parts, one for each index of `groups`. The reference program is written for one: setup_inputs(seed, part) draws one part's arguments, and reference() takes and returns one part's arrays. A program takes and returns all parts, laid end to end along the dimension named above; an argument that names none is the same for every part. Nothing has to cross between parts.
Inputs may be any that keep to these rules, and one draw needn't show every extreme that they name: `wave_slots`: each number of 0 to 511 stands in exactly one slot. `band_sizes`: the 16 sizes sum to 512. `vert_modes`: an orthonormal matrix.
All inputs are finite; a program needn't handle non-finite values.
Results may differ from the reference program's by a relative error of at most 0.011.
Values may be sent and summed in bfloat16 or wider, within the bound.
A program may use at most 192 MiB of HBM per device.

```python
import math
import jax
import jax.numpy as jnp
import numpy as np
from jax import lax

M = 512
NLAT = 512
NLON = 1024
FIELD_COUNT = 3
UNITS = 512
BANDS = 16
BAND_MOST = 64
LEVELS = 8
ENSEMBLE_SIZE = 2
FEAT = 24


def draw_vert_modes(key, part):
    raw_matrix = jax.random.normal(jax.random.fold_in(key, 11), (LEVELS, LEVELS), jnp.float32)
    orthonormal, upper_tri = jnp.linalg.qr(raw_matrix)
    return orthonormal.astype(jnp.float32)


def block_levels(own_key, extent, split, smallest, largest):
    def one(position, shards_of):
        heights = jax.random.uniform(jax.random.fold_in(jax.random.fold_in(own_key, 6), position), (shards_of,), jnp.float32, smallest / len(split), largest / len(split))
        return jnp.repeat(jnp.exp(heights), extent[position] // shards_of).reshape((-1,) + (1,) * (len(extent) - position - 1))

    level = one(*split[0])
    for cut in split[1:]:
        level = level * one(*cut)
    return level


def split_up(number_of, total, bound, slope):
    weights = [(1 << 20) // math.isqrt(standing ** slope) + 1 for standing in range(2, number_of + 1)]
    rest, holding = total - bound - (number_of - 1), [1] * (number_of - 1)
    while rest > 0:
        candidates = [i for i in range(number_of - 1) if holding[i] < bound]
        whole, budget = sum([weights[i] for i in candidates]), rest
        for i in candidates:
            extra = min(bound - holding[i], max(1, budget * weights[i] // whole), rest)
            holding[i] = holding[i] + extra
            rest = rest - extra
    return np.array([bound] + holding)


def ragged(stream_key, amount, total, bound, slope):
    if amount == 2:
        one = jax.random.randint(stream_key, (), max(1, total - bound), min(bound, total - 1) + 1)
        return jnp.stack([one, total - one])
    lengths = jnp.asarray(split_up(amount, total, bound, slope), jnp.int32)
    pairs = (amount - 1) // 2
    giver, taker = lengths[1:1 + 2 * pairs:2], lengths[2:2 + 2 * pairs:2]
    margin = jnp.minimum(giver - 1, bound - taker)
    passed = jax.random.randint(jax.random.fold_in(stream_key, 1), (pairs,), 0, 1 << 20) % (margin + 1)
    lengths = lengths.at[1:1 + 2 * pairs:2].set(giver - passed).at[2:2 + 2 * pairs:2].set(taker + passed)
    return lengths[jax.random.permutation(jax.random.fold_in(stream_key, 2), amount)]


def centred(own_key, shape, spread, reach, split=(), held_as=jnp.bfloat16):
    drawn = spread * jax.random.normal(own_key, shape, jnp.float32)
    if split:
        drawn = drawn * block_levels(own_key, shape, split, -0.22, 0.18)
    return jnp.clip(drawn, -reach, reach).astype(held_as)


def setup_inputs(seed: int = 0, part: int = 0) -> dict:
    key_list = jax.random.split(jax.random.key(seed), 12)
    own_keys = jax.random.split(jax.random.fold_in(key_list[11], part), 12)
    return {
        "grid_state": centred(own_keys[0], (ENSEMBLE_SIZE, FIELD_COUNT, LEVELS, NLAT, NLON), 1.0, 6.0, ((0, 2), (2, 2), (3, 4))),
        "wave_slots": jax.random.permutation(key_list[1], M).astype(jnp.int32),
        "lat_basis": centred(key_list[2], (M, M, NLAT), NLAT ** -0.5, 0.25, ((0, 8),)),
        "vert_modes": draw_vert_modes(jax.random.fold_in(key_list[11], 71), part),
        "vert_rates": jnp.clip(jnp.exp(jax.random.uniform(key_list[4], (FIELD_COUNT, LEVELS), jnp.float32, math.log(0.05), math.log(20.0))), 0.05, 20.0),
        "band_sizes": ragged(key_list[5], BANDS, NLAT, BAND_MOST, 2).astype(jnp.int32),
        "norm_gain": jnp.clip(1.0 + 0.15 * jax.random.normal(key_list[6], (FEAT,), jnp.float32), 0.25, 1.75),
        "w_in": centred(key_list[7], (UNITS, FEAT), FEAT ** -0.5, 1.25),
        "band_bias": centred(key_list[8], (UNITS, BANDS), 1.0, 6.0, (), jnp.float32),
        "w_mid": centred(key_list[9], (UNITS, UNITS), UNITS ** -0.5, 0.25),
        "w_out": centred(key_list[10], (FEAT, UNITS), UNITS ** -0.5, 0.25),
    }


transport_speed = 0.5
norm_eps = 1e-06

def fourier_tables(wave_slots, lon_count):
    wave_count = wave_slots.shape[0]
    longitude = jnp.arange(lon_count, dtype=jnp.int32)
    integer_phase = longitude[:, None] * wave_slots[None, :] % lon_count
    phase_angle = integer_phase.astype(jnp.float32) * (2.0 * math.pi / lon_count)
    table_scale = 1.0 / math.sqrt(lon_count)
    cosine = jnp.cos(phase_angle) * table_scale
    sine_part = jnp.sin(phase_angle) * table_scale
    forward = jnp.stack([cosine, -sine_part], axis=1).reshape(lon_count, 2 * wave_count).astype(jnp.bfloat16)
    weight = jnp.where(wave_slots == 0, 1.0, 2.0).astype(jnp.float32)
    inverse = jnp.stack([cosine.T * weight[:, None], -sine_part.T * weight[:, None]], axis=0).astype(jnp.bfloat16)
    return (forward, inverse)

def advection_term(padded, main_band_entries):
    above_main_entries = padded[:, :, :, 2:, :].astype(jnp.float32)
    below_main_entries = padded[:, :, :, :-2, :].astype(jnp.float32)
    oscillation_factor = jnp.roll(main_band_entries, -1, axis=1).astype(jnp.float32)
    return (main_band_entries.astype(jnp.float32) + transport_speed * oscillation_factor * (above_main_entries - below_main_entries)).astype(jnp.bfloat16)

def couple(spectra, wave_part, vert_modes, vert_rates):
    wave_count = spectra.shape[-1]
    degree = wave_part[:, None] + jnp.arange(wave_count, dtype=jnp.int32)[None, :]
    spectra = jnp.where((degree < wave_count)[:, None, None, None, None, :], spectra, 0.0)
    curvature = (degree * (degree + 1)).astype(jnp.float32) / float(wave_count * wave_count)
    vorticity = spectra[:, :, 0] / (1.0 + curvature[:, None, None, None, :] * vert_rates[0][None, None, :, None, None])
    coupled_part = spectra[:, :, 1:]
    modal = jnp.einsum('sbflrk,li->sbfirk', coupled_part, vert_modes, precision=lax.Precision.HIGHEST)
    scaled = modal / (1.0 + curvature[:, None, None, None, None, :] * vert_rates[1:][None, None, :, :, None, None])
    restored = jnp.einsum('sbfirk,li->sbflrk', scaled, vert_modes, precision=lax.Precision.HIGHEST)
    return jnp.concatenate([vorticity[:, :, None], restored], axis=2)

def column_net(grid_cols, lat_first, band_sizes, norm_gain, w_in, band_bias, w_mid, w_out):
    members, fields, levels, lat_rows, lon_cells = grid_cols.shape
    unit_count = w_in.shape[0]
    values = grid_cols.reshape(members, fields * levels, lat_rows * lon_cells).astype(jnp.float32)
    average_squared = lax.optimization_barrier(jnp.mean(values * values, axis=1, keepdims=True))
    rescaled_values = (values * lax.rsqrt(average_squared + norm_eps) * norm_gain[None, :, None]).astype(jnp.bfloat16)
    rescaled_values = lax.optimization_barrier(rescaled_values)
    band_ends = jnp.cumsum(band_sizes).astype(jnp.int32)
    band_starts = band_ends - band_sizes
    latitude = lat_first + jnp.arange(lat_rows, dtype=jnp.int32)
    inside = ((latitude[None, :] >= band_starts[:, None]) & (latitude[None, :] < band_ends[:, None])).astype(jnp.float32)
    lat_bias = jnp.dot(band_bias, inside, precision=lax.Precision.HIGHEST)
    cell_bias = jnp.broadcast_to(lat_bias[:, :, None], (unit_count, lat_rows, lon_cells)).reshape(unit_count, lat_rows * lon_cells)
    first_layer = jnp.einsum('hf,bfc->bhc', w_in.astype(jnp.float32), rescaled_values.astype(jnp.float32))
    first_layer = lax.optimization_barrier(jax.nn.silu(first_layer + cell_bias[None]).astype(jnp.bfloat16))
    second = jnp.einsum('hg,bgc->bhc', w_mid.astype(jnp.float32), first_layer.astype(jnp.float32))
    second = lax.optimization_barrier(jax.nn.silu(second).astype(jnp.bfloat16))
    increment = jnp.einsum('fh,bhc->bfc', w_out.astype(jnp.float32), second.astype(jnp.float32))
    return (values + increment).astype(jnp.bfloat16).reshape(grid_cols.shape)

def reference(grid_state, wave_slots, lat_basis, vert_modes, vert_rates, band_sizes, norm_gain, w_in, band_bias, w_mid, w_out):
    members, fields, levels, lat_count, lon_count = grid_state.shape
    wave_count = wave_slots.shape[0]
    slot_block = 8
    lat_block = 8
    padded = jnp.pad(grid_state, ((0, 0), (0, 0), (0, 0), (1, 1), (0, 0)))
    advected = advection_term(padded, grid_state)
    forward, inverse = fourier_tables(wave_slots, lon_count)
    coeffs = jnp.dot(advected.reshape(-1, lon_count).astype(jnp.float32), forward.astype(jnp.float32), preferred_element_type=jnp.float32).astype(jnp.bfloat16)
    coeffs = coeffs.reshape(members, fields, levels, lat_count, 2, wave_count)
    by_slot = jnp.moveaxis(coeffs, 5, 0).reshape(wave_count // slot_block, slot_block, members, fields, levels, lat_count, 2)
    basis_blocks = lat_basis.reshape(wave_count // slot_block, slot_block, wave_count, lat_count)
    wave_blocks = wave_slots.reshape(wave_count // slot_block, slot_block)

    def legendre(operands):
        basis_part, coeff_part, wave_part = operands
        raw_spectra = jnp.einsum('skj,sbfljr->sbflrk', basis_part.astype(jnp.float32), coeff_part.astype(jnp.float32))
        coupled = couple(raw_spectra, wave_part, vert_modes, vert_rates)
        rounded = lax.optimization_barrier(coupled.astype(jnp.bfloat16))
        back_part = jnp.einsum('skj,sbflrk->sbflrj', basis_part.astype(jnp.float32), rounded.astype(jnp.float32))
        return (coupled, back_part.astype(jnp.bfloat16))
    coupled_blocks, back_blocks = lax.map(legendre, (basis_blocks, by_slot, wave_blocks))
    spectral = coupled_blocks.reshape(wave_count, members, fields, levels, 2, wave_count)
    back_fourier = back_blocks.reshape(wave_count, members, fields, levels, 2, lat_count)
    grid_mid = jnp.einsum('pbflrj,rpi->bflji', back_fourier.astype(jnp.float32), inverse.astype(jnp.float32)).astype(jnp.bfloat16)
    lat_blocks = grid_mid.reshape(members, fields, levels, lat_count // lat_block, lat_block, lon_count)
    lat_blocks = jnp.moveaxis(lat_blocks, 3, 0)
    starts = jnp.arange(lat_count // lat_block, dtype=jnp.int32) * lat_block

    def net_block(operands):
        lat_slab, slab_start = operands
        return column_net(lat_slab, slab_start, band_sizes, norm_gain, w_in, band_bias, w_mid, w_out)
    mixed_slabs = lax.map(net_block, (lat_blocks, starts))
    new_state = jnp.moveaxis(mixed_slabs, 0, 3).reshape(members, fields, levels, lat_count, lon_count)
    return (spectral, new_state)
```

```python
import functools
import math

import jax
import jax.numpy as jnp
from jax import lax
from jax.experimental import pallas as pl
from jax.experimental.pallas import tpu as pltpu
from jax.sharding import PartitionSpec as P

transport_speed = 0.5
norm_eps = 1e-06
lane = 128
mesh_id = pl.DeviceIdType.MESH
vmem_limit = 60 * 1024 * 1024


def extended(array, sides, width):
    for axis, dim in sides:
        size, length = (lax.axis_size(axis), array.shape[dim])
        up = [(i, (i + 1) % size) for i in range(size - 1)]
        down = [(j, i) for i, j in up]
        last = lax.slice_in_dim(array, length - width, length, axis=dim)
        initial = lax.slice_in_dim(array, 0, width, axis=dim)
        before = lax.ppermute(last, axis, up)
        after = lax.ppermute(initial, axis, down)
        array = jnp.concatenate([before, array, after], axis=dim)
    return array


def advection_term(padded, main_band_entries):
    above_main_entries = padded[:, :, :, 2:, :].astype(jnp.float32)
    below_main_entries = padded[:, :, :, :-2, :].astype(jnp.float32)
    oscillation_factor = jnp.roll(main_band_entries, -1, axis=1).astype(jnp.float32)
    return (
        main_band_entries.astype(jnp.float32)
        + transport_speed * oscillation_factor * (above_main_entries - below_main_entries)
    ).astype(jnp.bfloat16)


def couple(spectra, wave_part, vert_modes, vert_rates):
    wave_count = spectra.shape[-1]
    degree = wave_part[:, None] + jnp.arange(wave_count, dtype=jnp.int32)[None, :]
    spectra = jnp.where((degree < wave_count)[:, None, None, None, None, :], spectra, 0.0)
    curvature = (degree * (degree + 1)).astype(jnp.float32) / float(wave_count * wave_count)
    vorticity = spectra[:, :, 0] / (
        1.0 + curvature[:, None, None, None, :] * vert_rates[0][None, None, :, None, None]
    )
    coupled_part = spectra[:, :, 1:]
    modal = jnp.einsum(
        "sbflrk,li->sbfirk", coupled_part, vert_modes, precision=lax.Precision.HIGHEST
    )
    scaled = modal / (
        1.0 + curvature[:, None, None, None, None, :] * vert_rates[1:][None, None, :, :, None, None]
    )
    restored = jnp.einsum("sbfirk,li->sbflrk", scaled, vert_modes, precision=lax.Precision.HIGHEST)
    return jnp.concatenate([vorticity[:, :, None], restored], axis=2)


def device_at(index, lev_count):
    return {"wide": index // lev_count, "lev": lax.rem(index, lev_count)}


def greet(me, count, lev_count):
    barrier = pltpu.get_barrier_semaphore()

    @pl.loop(1, count)
    def _(k):
        peer = lax.rem(me + k, count)
        pl.semaphore_signal(
            barrier, inc=1, device_id=device_at(peer, lev_count), device_id_type=mesh_id
        )

    pl.semaphore_wait(barrier, count - 1)


def phase_factors(wave_slots, block_count, lon_count):
    waves = wave_slots.reshape(block_count, 1, -1)

    def angle(steps):
        phase = waves[..., None] * steps % lon_count
        return phase.astype(jnp.float32) * (2.0 * math.pi / lon_count)

    coarse = angle(jnp.arange(lon_count // lane, dtype=jnp.int32) * lane)
    fine = angle(jnp.arange(lane, dtype=jnp.int32))
    scale = 1.0 / math.sqrt(lon_count)
    cos_a, sin_a = (jnp.cos(coarse) * scale, jnp.sin(coarse) * scale)
    p = jnp.concatenate([cos_a, -sin_a], axis=1)
    q = jnp.concatenate([-sin_a, -cos_a], axis=1)
    both = lambda value: jnp.concatenate([value, value], axis=1)
    flat = lambda value: value.reshape(2 * wave_slots.shape[0], -1)
    return (flat(p), flat(q), flat(both(jnp.cos(fine))), flat(both(jnp.sin(fine))))


def forward_kernel(p_ref, q_ref, cos_ref, sin_ref, adv_ref, out_ref, table_ref):
    @pl.when(pl.program_id(0) == 0)
    def _():
        rows = 256

        @pl.loop(0, table_ref.shape[0] // rows)
        def _(step):
            here = pl.ds(pl.multiple_of(step * rows, rows), rows)
            cos_b, sin_b = (cos_ref[here, :], sin_ref[here, :])
            p, q = (p_ref[here, :], q_ref[here, :])
            for a in range(p_ref.shape[1]):
                table_ref[here, a * lane : (a + 1) * lane] = (
                    p[:, a : a + 1] * cos_b + q[:, a : a + 1] * sin_b
                ).astype(jnp.bfloat16)

    group, lat_rows, lon_count = adv_ref.shape
    blocks, _, width, _ = out_ref.shape
    result = lax.dot_general(
        table_ref[...],
        adv_ref[...].reshape(group * lat_rows, lon_count),
        (((1,), (1,)), ((), ())),
        preferred_element_type=jnp.float32,
    ).astype(jnp.bfloat16)
    for g in range(group):
        out_ref[:, g] = result[:, g * lat_rows : (g + 1) * lat_rows].reshape(
            blocks, width, lat_rows
        )


def forward_dft(advected, wave_slots, block_count):
    layers, lat_rows, lon_count = advected.shape
    factors = phase_factors(wave_slots, block_count, lon_count)
    rows = factors[0].shape[0]
    width = rows // block_count
    group = 2 if lat_rows % lane == 0 and layers % 2 == 0 else 1
    whole = lambda value: pl.BlockSpec(value.shape, lambda i: (0, 0))
    return pl.pallas_call(
        forward_kernel,
        grid=(layers // group,),
        in_specs=[whole(value) for value in factors]
        + [pl.BlockSpec((group, lat_rows, lon_count), lambda i: (i, 0, 0))],
        out_specs=[
            pl.BlockSpec((block_count, group, width, lat_rows), lambda i: (0, i, 0, 0)),
            pl.BlockSpec((rows, lon_count), lambda i: (0, 0)),
        ],
        out_shape=[
            jax.ShapeDtypeStruct((block_count, layers, width, lat_rows), jnp.bfloat16),
            jax.ShapeDtypeStruct((rows, lon_count), jnp.bfloat16),
        ],
        compiler_params=pltpu.CompilerParams(vmem_limit_bytes=vmem_limit),
        name="forward_dft",
    )(*factors, advected)


def exchange_kernel(count, lev_count, src_ref, dst_ref, send_sem, recv_sem, own_sem):
    me = lax.axis_index("wide") * lev_count + lax.axis_index("lev")
    greet(me, count, lev_count)
    own = pltpu.make_async_copy(src_ref.at[me], dst_ref.at[me], own_sem)

    def outgoing(k):
        peer = lax.rem(me + k, count)
        return pltpu.make_async_remote_copy(
            src_ref=src_ref.at[peer],
            dst_ref=dst_ref.at[me],
            send_sem=send_sem.at[k],
            recv_sem=recv_sem.at[k],
            device_id=device_at(peer, lev_count),
            device_id_type=mesh_id,
        )

    @pl.loop(1, count)
    def _(k):
        outgoing(k).start()

    own.start()
    own.wait()

    @pl.loop(1, count)
    def _(k):
        outgoing(k).wait_recv()

    @pl.loop(1, count)
    def _(k):
        outgoing(k).wait_send()


def exchange(parcels, lev_count):
    count = parcels.shape[0]
    return pl.pallas_call(
        functools.partial(exchange_kernel, count, lev_count),
        out_shape=jax.ShapeDtypeStruct(parcels.shape, parcels.dtype),
        in_specs=[pl.BlockSpec(memory_space=pl.ANY)],
        out_specs=pl.BlockSpec(memory_space=pltpu.VMEM),
        scratch_shapes=[
            pltpu.SemaphoreType.DMA((count,)),
            pltpu.SemaphoreType.DMA((count,)),
            pltpu.SemaphoreType.DMA,
        ],
        compiler_params=pltpu.CompilerParams(
            collective_id=0, has_side_effects=True, vmem_limit_bytes=vmem_limit
        ),
        name="exchange",
    )(parcels)


def column_kernel(
    lev_count,
    row_count,
    src_ref,
    table_ref,
    hot_ref,
    gain_ref,
    w_first_ref,
    w_mid_ref,
    w_out_ref,
    out_ref,
    land_ref,
    x_ref,
    y_ref,
    send_sem,
    recv_sem,
    own_sem,
):
    chunks, count, tall, width = land_ref.shape
    feat = gain_ref.shape[0]
    lon_count = table_ref.shape[1]
    me = lax.axis_index("wide") * lev_count + lax.axis_index("lev")
    greet(me, count, lev_count)

    def outgoing(c, k):
        peer = lax.rem(me + k, count)
        return pltpu.make_async_remote_copy(
            src_ref=src_ref.at[peer, c],
            dst_ref=land_ref.at[c, me],
            send_sem=send_sem.at[c, k],
            recv_sem=recv_sem.at[c, k],
            device_id=device_at(peer, lev_count),
            device_id_type=mesh_id,
        )

    def own(c):
        return pltpu.make_async_copy(src_ref.at[me, c], land_ref.at[c, me], own_sem.at[c])

    @pl.loop(0, chunks)
    def _(c):
        @pl.loop(1, count)
        def _(k):
            outgoing(c, k).start()

        own(c).start()

    @pl.loop(0, chunks)
    def _(c):
        own(c).wait()

        @pl.loop(1, count)
        def _(k):
            outgoing(c, k).wait_recv()

        if width % lane == 0:
            columns = jnp.concatenate([land_ref[c, d] for d in range(count)], axis=1)
            x_ref[...] = jnp.dot(columns, table_ref[...], preferred_element_type=jnp.float32)
        else:
            x_ref[...] = jnp.zeros_like(x_ref)

            @pl.loop(0, count)
            def _(d):
                here = pl.ds(pl.multiple_of(d * width, width), width)
                x_ref[...] += jnp.dot(
                    land_ref[c, d], table_ref[here, :], preferred_element_type=jnp.float32
                )

        piece = lon_count // 2

        group = 4 if width % lane == 0 and row_count % 4 == 0 else 1
        halves = lon_count // piece

        @pl.loop(0, row_count // group)
        def _(step_row):
            held = {}

            def place(unit):
                j = step_row * group + unit // halves
                start = unit % halves * piece
                return j, pl.ds(pl.multiple_of(j * feat, 8), feat), slice(start, start + piece)

            def enter(unit):
                j, rows, here = place(unit)
                hot = hot_ref[c * row_count + j]
                hot = jnp.concatenate([hot] * (piece // lane), axis=1)
                x = x_ref[rows, here].astype(jnp.bfloat16).astype(jnp.float32)
                average = jnp.sum(x * x, axis=0, keepdims=True) * (1.0 / feat)
                normed = x * lax.rsqrt(average + norm_eps) * gain_ref[...]
                entries = jnp.concatenate([normed, hot], axis=0).astype(jnp.bfloat16)
                half = jnp.dot(w_first_ref[...], entries, preferred_element_type=jnp.float32)
                held["x", unit] = x
                held["in", unit] = half.astype(jnp.bfloat16)

            def middle(unit):
                half = held.pop(("in", unit))
                first = half * jnp.tanh(half) + half
                half = jnp.dot(w_mid_ref[...], first, preferred_element_type=jnp.float32)
                held["mid", unit] = half.astype(jnp.bfloat16)

            def leave(unit):
                j, _, here = place(unit)
                half = held.pop(("mid", unit))
                second = half * jnp.tanh(half) + half
                y_ref[j, :, here] = held.pop(("x", unit)) + jnp.dot(
                    w_out_ref[...], second, preferred_element_type=jnp.float32
                )

            units = group * halves
            for step in range(units + 2):
                for late, stage in ((0, enter), (1, middle), (2, leave)):
                    if 0 <= step - late < units:
                        stage(step - late)

        out_ref[:, pl.ds(pl.multiple_of(c * row_count, row_count), row_count), :] = jnp.swapaxes(
            y_ref[...], 0, 1
        ).astype(jnp.bfloat16)

    @pl.loop(0, chunks)
    def _(c):
        @pl.loop(1, count)
        def _(k):
            outgoing(c, k).wait_send()


def back_and_columns(parcels, table, hot, norm_gain, w_first, w_mid, w_out, lev_count, row_count):
    count, chunks, tall, width = parcels.shape
    feat = norm_gain.shape[0]
    lon_count = table.shape[1]
    vmem = pl.BlockSpec(memory_space=pltpu.VMEM)
    return pl.pallas_call(
        functools.partial(column_kernel, lev_count, row_count),
        out_shape=jax.ShapeDtypeStruct((feat, chunks * row_count, lon_count), jnp.bfloat16),
        in_specs=[pl.BlockSpec(memory_space=pl.ANY)] + [vmem] * 6,
        out_specs=vmem,
        scratch_shapes=[
            pltpu.VMEM((chunks, count, tall, width), jnp.bfloat16),
            pltpu.VMEM((tall, lon_count), jnp.float32),
            pltpu.VMEM((row_count, feat, lon_count), jnp.float32),
            pltpu.SemaphoreType.DMA((chunks, count)),
            pltpu.SemaphoreType.DMA((chunks, count)),
            pltpu.SemaphoreType.DMA((chunks,)),
        ],
        compiler_params=pltpu.CompilerParams(
            collective_id=1, has_side_effects=True, vmem_limit_bytes=vmem_limit
        ),
        name="back_and_columns",
    )(parcels, table, hot, norm_gain[:, None], w_first, w_mid, w_out)


def legendre_kernel(
    lev_count, land_ref, basis_ref, wave_ref, modes_ref, turned_ref, rates_ref, out_ref, back_ref,
    x_ref,
):
    count, layers, _, slots, lat_dev = land_ref.shape
    wide_count = count // lev_count
    _, fields, levels, _, wave_count = out_ref.shape
    lev_dev = layers // fields
    for w in range(wide_count):
        pieces = []
        for f in range(fields):
            for r in range(2):
                rows = jnp.concatenate(
                    [
                        land_ref[w * lev_count + l, f * lev_dev : (f + 1) * lev_dev, r]
                        for l in range(lev_count)
                    ],
                    axis=0,
                ).astype(jnp.float32)
                pieces.append(jnp.swapaxes(rows, 0, 1))
        x_ref[:, :, w * lat_dev : (w + 1) * lat_dev] = jnp.concatenate(pieces, axis=1).astype(
            jnp.bfloat16
        )
    position = lax.broadcasted_iota(jnp.int32, (1, wave_count), 1)

    def mixed(value, columns):
        total = columns[:, 0:1] * value[0:1, :]
        for l in range(1, levels):
            total = total + columns[:, l : l + 1] * value[l : l + 1, :]
        return total

    for s in range(slots):
        basis = basis_ref[s]
        raw = lax.dot_general(
            x_ref[s], basis, (((1,), (1,)), ((), ())), preferred_element_type=jnp.float32
        )
        wave = wave_ref[s : s + 1, 0:1]
        degree = wave + position
        raw = jnp.where(degree < wave_count, raw, 0.0)
        curvature = (degree * (degree + 1)).astype(jnp.float32) * (
            1.0 / float(wave_count * wave_count)
        )
        weight = jnp.where(wave == 0, 1.0, 2.0)
        parts = []
        for f in range(fields):
            scale = 1.0 / (1.0 + curvature * rates_ref[f])
            for r in range(2):
                first = (f * 2 + r) * levels
                value = raw[first : first + levels]
                if f == 0:
                    value = value * scale
                else:
                    value = mixed(mixed(value, turned_ref[...]) * scale, modes_ref[...])
                out_ref[s, f, :, r, :] = value
                parts.append(value)
        rounded = jnp.concatenate(parts, axis=0).astype(jnp.bfloat16)
        back = jnp.dot(rounded, basis, preferred_element_type=jnp.float32) * weight
        for r in range(2):
            back_ref[r, s] = jnp.concatenate(
                [
                    back[(f * 2 + r) * levels : (f * 2 + r + 1) * levels]
                    for f in range(fields)
                ],
                axis=0,
            ).astype(jnp.bfloat16)


def legendre(arrived, lat_basis, wave_part, vert_modes, vert_rates, lev_count, slots):
    slot_dev, wave_count, lat_count = lat_basis.shape
    count, layers, _, lat_dev = arrived.shape
    fields, levels = vert_rates.shape
    whole = lambda shape: pl.BlockSpec(shape, lambda i: (0,) * len(shape))
    return pl.pallas_call(
        functools.partial(legendre_kernel, lev_count),
        grid=(slot_dev // slots,),
        in_specs=[
            pl.BlockSpec((count, layers, 2, slots, lat_dev), lambda i: (0, 0, 0, i, 0)),
            pl.BlockSpec((slots, wave_count, lat_count), lambda i: (i, 0, 0)),
            pl.BlockSpec((slots, lane), lambda i: (i, 0)),
            whole((levels, levels)),
            whole((levels, levels)),
            whole((fields, levels, 1)),
        ],
        out_specs=[
            pl.BlockSpec((slots, fields, levels, 2, wave_count), lambda i: (i, 0, 0, 0, 0)),
            pl.BlockSpec((2, slots, fields * levels, lat_count), lambda i: (0, i, 0, 0)),
        ],
        out_shape=[
            jax.ShapeDtypeStruct((slot_dev, fields, levels, 2, wave_count), jnp.float32),
            jax.ShapeDtypeStruct((2, slot_dev, fields * levels, lat_count), jnp.bfloat16),
        ],
        scratch_shapes=[pltpu.VMEM((slots, 2 * fields * levels, lat_count), jnp.bfloat16)],
        compiler_params=pltpu.CompilerParams(vmem_limit_bytes=vmem_limit),
        name="legendre",
    )(
        arrived.reshape(count, layers, 2, slot_dev, lat_dev),
        lat_basis,
        jnp.broadcast_to(wave_part[:, None], (slot_dev, lane)),
        vert_modes,
        vert_modes.T,
        vert_rates[:, :, None],
    )


def legendre_plain(arrived, lat_basis, wave_part, vert_modes, vert_rates, wide_count, lev_count):
    slot_dev, wave_count, lat_count = lat_basis.shape
    _, layers, _, lat_dev = arrived.shape
    fields, levels = vert_rates.shape
    by_wave = arrived.reshape(
        wide_count, lev_count, fields, levels // lev_count, 2, slot_dev, lat_dev
    )
    by_wave = by_wave.transpose(5, 4, 2, 1, 3, 0, 6).reshape(
        slot_dev, 2, 1, fields, levels, lat_count
    )
    raw_spectra = jnp.einsum(
        "skj,srbflj->sbflrk", lat_basis, by_wave, preferred_element_type=jnp.float32
    )
    spectral = couple(raw_spectra, wave_part, vert_modes, vert_rates)
    weight = jnp.where(wave_part == 0, 1.0, 2.0).astype(jnp.bfloat16)
    back_coeffs = jnp.einsum(
        "skj,sbflrk->srbflj",
        lat_basis,
        spectral.astype(jnp.bfloat16),
        preferred_element_type=jnp.float32,
    ).astype(jnp.bfloat16)
    back_coeffs = back_coeffs * weight[:, None, None, None, None, None]
    back = back_coeffs.transpose(1, 0, 2, 3, 4, 5).reshape(
        2, slot_dev, fields * levels, lat_count
    )
    return (spectral[:, 0], back)


def band_rows(lat_first, lat_rows, band_sizes, band_bias, w_in):
    feat, bands = (w_in.shape[1], band_sizes.shape[0])
    band_ends = jnp.cumsum(band_sizes)
    band_starts = band_ends - band_sizes
    latitude = lat_first + jnp.arange(lat_rows, dtype=jnp.int32)
    inside = (
        (latitude[:, None] >= band_starts[None, :]) & (latitude[:, None] < band_ends[None, :])
    ).astype(jnp.float32)
    spare = -(feat + 2 * bands) % 16
    hot = jnp.pad(jnp.concatenate([inside, inside], axis=1), ((0, 0), (0, spare)))
    hot = jnp.broadcast_to(hot[:, :, None], hot.shape + (lane,))
    high = band_bias.astype(jnp.bfloat16)
    low = (band_bias - high.astype(jnp.float32)).astype(jnp.bfloat16)
    w_first = jnp.pad(jnp.concatenate([w_in, high, low], axis=1), ((0, 0), (0, spare)))
    return (hot, w_first * jnp.bfloat16(0.5))


def local(
    grid_state,
    wave_slots,
    lat_basis,
    vert_modes,
    vert_rates,
    band_sizes,
    norm_gain,
    w_in,
    band_bias,
    w_mid,
    w_out,
):
    members, fields, lev_dev, lat_dev, lon_count = grid_state.shape
    wide_count = lax.axis_size("wide")
    lev_count = lax.axis_size("lev")
    count = wide_count * lev_count
    slot_dev, wave_count, lat_count = lat_basis.shape
    levels = lev_dev * lev_count
    block_index = lax.axis_index("wide") * lev_count + lax.axis_index("lev")
    wave_part = lax.dynamic_slice_in_dim(wave_slots, block_index * slot_dev, slot_dev)

    padded = extended(grid_state, (("wide", 3),), 1)
    advected = advection_term(padded, grid_state)
    layers = members * fields * lev_dev
    coeffs, table = forward_dft(
        advected.reshape(layers, lat_dev, lon_count), wave_slots, count
    )
    arrived = exchange(coeffs, lev_count)
    slots = 8
    if lat_dev % lane == 0 and slot_dev % slots == 0 and levels == slots:
        spectral, back = legendre(
            arrived, lat_basis, wave_part, vert_modes, vert_rates, lev_count, slots
        )
    else:
        spectral, back = legendre_plain(
            arrived, lat_basis, wave_part, vert_modes, vert_rates, wide_count, lev_count
        )
    spectral = spectral[:, None]
    lat_part = lat_count // count
    feat = fields * levels
    row_count = 8 if lat_part % 8 == 0 else lat_part
    turned = lax.optimization_barrier(
        back.reshape(2 * slot_dev, feat, lat_count)
    )
    parcels = turned.transpose(2, 1, 0).reshape(
        count, lat_part // row_count, row_count * feat, 2 * slot_dev
    )
    hot, w_first = band_rows(block_index * lat_part, lat_part, band_sizes, band_bias, w_in)
    half_mid = w_mid * jnp.bfloat16(0.5)
    new_state = back_and_columns(
        parcels, table, hot, norm_gain, w_first, half_mid, w_out, lev_count, row_count
    ).reshape(members, fields, levels, lat_part, lon_count)
    return (spectral, new_state)


def solution(mesh):
    placed = (
        P(("groups", "fld"), None, "lev", "wide", None),
        P(),
        P(("wide", "lev"), None, None),
        P(),
        P(),
        P(),
        P(),
        P(),
        P(),
        P(),
        P(),
    )
    return jax.shard_map(
        local,
        mesh=mesh,
        in_specs=placed,
        out_specs=(
            P(("wide", "lev"), ("groups", "fld"), None, None, None, None),
            P(("groups", "fld"), None, None, ("wide", "lev"), None),
        ),
        check_vma=False,
    )
```

```python
import functools
import math

import jax
import jax.numpy as jnp
from jax import lax
from jax.experimental import pallas as pl
from jax.experimental.pallas import tpu as pltpu
from jax.sharding import PartitionSpec as P

transport_speed = 0.5
norm_eps = 1e-06
lane = 128
mesh_id = pl.DeviceIdType.MESH
vmem_limit = 60 * 1024 * 1024


def edges(array, axis, dim):
    size, length = (lax.axis_size(axis), array.shape[dim])
    up = [(i, i + 1) for i in range(size - 1)]
    down = [(j, i) for i, j in up]
    last = lax.slice_in_dim(array, length - 1, length, axis=dim)
    initial = lax.slice_in_dim(array, 0, 1, axis=dim)
    return (lax.ppermute(last, axis, up), lax.ppermute(initial, axis, down))


def advection_term(padded, main_band_entries):
    above_main_entries = padded[:, :, :, 2:, :].astype(jnp.float32)
    below_main_entries = padded[:, :, :, :-2, :].astype(jnp.float32)
    oscillation_factor = jnp.roll(main_band_entries, -1, axis=1).astype(jnp.float32)
    return (
        main_band_entries.astype(jnp.float32)
        + transport_speed * oscillation_factor * (above_main_entries - below_main_entries)
    ).astype(jnp.bfloat16)


def couple(spectra, wave_part, vert_modes, vert_rates):
    wave_count = spectra.shape[-1]
    degree = wave_part[:, None] + jnp.arange(wave_count, dtype=jnp.int32)[None, :]
    spectra = jnp.where((degree < wave_count)[:, None, None, None, None, :], spectra, 0.0)
    curvature = (degree * (degree + 1)).astype(jnp.float32) / float(wave_count * wave_count)
    vorticity = spectra[:, :, 0] / (
        1.0 + curvature[:, None, None, None, :] * vert_rates[0][None, None, :, None, None]
    )
    coupled_part = spectra[:, :, 1:]
    modal = jnp.einsum(
        "sbflrk,li->sbfirk", coupled_part, vert_modes, precision=lax.Precision.HIGHEST
    )
    scaled = modal / (
        1.0 + curvature[:, None, None, None, None, :] * vert_rates[1:][None, None, :, :, None, None]
    )
    restored = jnp.einsum("sbfirk,li->sbflrk", scaled, vert_modes, precision=lax.Precision.HIGHEST)
    return jnp.concatenate([vorticity[:, :, None], restored], axis=2)


def device_at(index, lev_count):
    return {"wide": index // lev_count, "lev": lax.rem(index, lev_count)}


def greet(me, count, lev_count):
    barrier = pltpu.get_barrier_semaphore()

    @pl.loop(1, count)
    def _(k):
        peer = lax.rem(me + k, count)
        pl.semaphore_signal(
            barrier, inc=1, device_id=device_at(peer, lev_count), device_id_type=mesh_id
        )

    pl.semaphore_wait(barrier, count - 1)


def phase_factors(wave_slots, block_count, lon_count):
    waves = wave_slots.reshape(block_count, 1, -1)

    def angle(steps):
        phase = waves[..., None] * steps % lon_count
        return phase.astype(jnp.float32) * (2.0 * math.pi / lon_count)

    coarse = angle(jnp.arange(lon_count // lane, dtype=jnp.int32) * lane)
    fine = angle(jnp.arange(lane, dtype=jnp.int32))
    scale = 1.0 / math.sqrt(lon_count)
    cos_a, sin_a = (jnp.cos(coarse) * scale, jnp.sin(coarse) * scale)
    p = jnp.concatenate([cos_a, -sin_a], axis=1)
    q = jnp.concatenate([-sin_a, -cos_a], axis=1)
    both = lambda value: jnp.concatenate([value, value], axis=1)
    flat = lambda value: value.reshape(2 * wave_slots.shape[0], -1)
    return (flat(p), flat(q), flat(both(jnp.cos(fine))), flat(both(jnp.sin(fine))))


def forward_kernel(p_ref, q_ref, cos_ref, sin_ref, adv_ref, out_ref, table_ref):
    @pl.when(pl.program_id(0) == 0)
    def _():
        rows = 256

        @pl.loop(0, table_ref.shape[0] // rows)
        def _(step):
            here = pl.ds(pl.multiple_of(step * rows, rows), rows)
            cos_b, sin_b = (cos_ref[here, :], sin_ref[here, :])
            p, q = (p_ref[here, :], q_ref[here, :])
            for a in range(p_ref.shape[1]):
                table_ref[here, a * lane : (a + 1) * lane] = (
                    p[:, a : a + 1] * cos_b + q[:, a : a + 1] * sin_b
                ).astype(jnp.bfloat16)

    group, lat_rows, lon_count = adv_ref.shape
    blocks, _, width, _ = out_ref.shape
    result = lax.dot_general(
        table_ref[...],
        adv_ref[...].reshape(group * lat_rows, lon_count),
        (((1,), (1,)), ((), ())),
        preferred_element_type=jnp.float32,
    ).astype(jnp.bfloat16)
    for g in range(group):
        out_ref[:, g] = result[:, g * lat_rows : (g + 1) * lat_rows].reshape(
            blocks, width, lat_rows
        )


def forward_dft(advected, wave_slots, block_count):
    layers, lat_rows, lon_count = advected.shape
    factors = phase_factors(wave_slots, block_count, lon_count)
    rows = factors[0].shape[0]
    width = rows // block_count
    group = 2 if lat_rows % lane == 0 and layers % 2 == 0 else 1
    whole = lambda value: pl.BlockSpec(value.shape, lambda i: (0, 0))
    return pl.pallas_call(
        forward_kernel,
        grid=(layers // group,),
        in_specs=[whole(value) for value in factors]
        + [pl.BlockSpec((group, lat_rows, lon_count), lambda i: (i, 0, 0))],
        out_specs=[
            pl.BlockSpec((block_count, group, width, lat_rows), lambda i: (0, i, 0, 0)),
            pl.BlockSpec((rows, lon_count), lambda i: (0, 0)),
        ],
        out_shape=[
            jax.ShapeDtypeStruct((block_count, layers, width, lat_rows), jnp.bfloat16),
            jax.ShapeDtypeStruct((rows, lon_count), jnp.bfloat16),
        ],
        compiler_params=pltpu.CompilerParams(vmem_limit_bytes=vmem_limit),
        name="forward_dft",
    )(*factors, advected)


def exchange_kernel(count, lev_count, src_ref, dst_ref, send_sem, recv_sem, own_sem):
    me = lax.axis_index("wide") * lev_count + lax.axis_index("lev")
    greet(me, count, lev_count)
    own = pltpu.make_async_copy(src_ref.at[me], dst_ref.at[me], own_sem)

    def outgoing(k):
        peer = lax.rem(me + k, count)
        return pltpu.make_async_remote_copy(
            src_ref=src_ref.at[peer],
            dst_ref=dst_ref.at[me],
            send_sem=send_sem.at[k],
            recv_sem=recv_sem.at[k],
            device_id=device_at(peer, lev_count),
            device_id_type=mesh_id,
        )

    @pl.loop(1, count)
    def _(k):
        outgoing(k).start()

    own.start()
    own.wait()

    @pl.loop(1, count)
    def _(k):
        outgoing(k).wait_recv()

    @pl.loop(1, count)
    def _(k):
        outgoing(k).wait_send()


def exchange(parcels, lev_count):
    count = parcels.shape[0]
    return pl.pallas_call(
        functools.partial(exchange_kernel, count, lev_count),
        out_shape=jax.ShapeDtypeStruct(parcels.shape, parcels.dtype),
        in_specs=[pl.BlockSpec(memory_space=pl.ANY)],
        out_specs=pl.BlockSpec(memory_space=pltpu.VMEM),
        scratch_shapes=[
            pltpu.SemaphoreType.DMA((count,)),
            pltpu.SemaphoreType.DMA((count,)),
            pltpu.SemaphoreType.DMA,
        ],
        compiler_params=pltpu.CompilerParams(
            collective_id=0, has_side_effects=True, vmem_limit_bytes=vmem_limit
        ),
        name="exchange",
    )(parcels)


def column_kernel(
    lev_count,
    row_count,
    src_ref,
    table_ref,
    hot_ref,
    gain_ref,
    w_first_ref,
    w_mid_ref,
    w_out_ref,
    out_ref,
    land_ref,
    x_ref,
    y_ref,
    send_sem,
    recv_sem,
    own_sem,
):
    chunks, count, tall, width = land_ref.shape
    feat = gain_ref.shape[0]
    lon_count = table_ref.shape[1]
    me = lax.axis_index("wide") * lev_count + lax.axis_index("lev")
    greet(me, count, lev_count)

    def outgoing(c, k):
        peer = lax.rem(me + k, count)
        return pltpu.make_async_remote_copy(
            src_ref=src_ref.at[peer, c],
            dst_ref=land_ref.at[c, me],
            send_sem=send_sem.at[c, k],
            recv_sem=recv_sem.at[c, k],
            device_id=device_at(peer, lev_count),
            device_id_type=mesh_id,
        )

    def own(c):
        return pltpu.make_async_copy(src_ref.at[me, c], land_ref.at[c, me], own_sem.at[c])

    @pl.loop(0, chunks)
    def _(c):
        @pl.loop(1, count)
        def _(k):
            outgoing(c, k).start()

        own(c).start()

    @pl.loop(0, chunks)
    def _(c):
        own(c).wait()

        @pl.loop(1, count)
        def _(k):
            outgoing(c, k).wait_recv()

        if width % lane == 0:
            columns = jnp.concatenate([land_ref[c, d] for d in range(count)], axis=1)
            x_ref[...] = jnp.dot(columns, table_ref[...], preferred_element_type=jnp.float32)
        else:
            x_ref[...] = jnp.zeros_like(x_ref)

            @pl.loop(0, count)
            def _(d):
                here = pl.ds(pl.multiple_of(d * width, width), width)
                x_ref[...] += jnp.dot(
                    land_ref[c, d], table_ref[here, :], preferred_element_type=jnp.float32
                )

        piece = lon_count // 2

        group = 4 if width % lane == 0 and row_count % 4 == 0 else 1
        halves = lon_count // piece

        @pl.loop(0, row_count // group)
        def _(step_row):
            held = {}

            def place(unit):
                j = step_row * group + unit // halves
                start = unit % halves * piece
                return j, pl.ds(pl.multiple_of(j * feat, 8), feat), slice(start, start + piece)

            def enter(unit):
                j, rows, here = place(unit)
                hot = hot_ref[c * row_count + j]
                hot = jnp.concatenate([hot] * (piece // lane), axis=1)
                x = x_ref[rows, here].astype(jnp.bfloat16).astype(jnp.float32)
                average = jnp.sum(x * x, axis=0, keepdims=True) * (1.0 / feat)
                normed = x * lax.rsqrt(average + norm_eps) * gain_ref[...]
                entries = jnp.concatenate([normed, hot], axis=0).astype(jnp.bfloat16)
                half = jnp.dot(w_first_ref[...], entries, preferred_element_type=jnp.float32)
                held["x", unit] = x
                held["in", unit] = half.astype(jnp.bfloat16)

            def middle(unit):
                half = held.pop(("in", unit))
                first = half * jnp.tanh(half) + half
                half = jnp.dot(w_mid_ref[...], first, preferred_element_type=jnp.float32)
                held["mid", unit] = half.astype(jnp.bfloat16)

            def leave(unit):
                j, _, here = place(unit)
                half = held.pop(("mid", unit))
                second = half * jnp.tanh(half) + half
                y_ref[j, :, here] = held.pop(("x", unit)) + jnp.dot(
                    w_out_ref[...], second, preferred_element_type=jnp.float32
                )

            units = group * halves
            for step in range(units + 2):
                for late, stage in ((0, enter), (1, middle), (2, leave)):
                    if 0 <= step - late < units:
                        stage(step - late)

        out_ref[:, pl.ds(pl.multiple_of(c * row_count, row_count), row_count), :] = jnp.swapaxes(
            y_ref[...], 0, 1
        ).astype(jnp.bfloat16)

    @pl.loop(0, chunks)
    def _(c):
        @pl.loop(1, count)
        def _(k):
            outgoing(c, k).wait_send()


def back_and_columns(parcels, table, hot, norm_gain, w_first, w_mid, w_out, lev_count, row_count):
    count, chunks, tall, width = parcels.shape
    feat = norm_gain.shape[0]
    lon_count = table.shape[1]
    vmem = pl.BlockSpec(memory_space=pltpu.VMEM)
    return pl.pallas_call(
        functools.partial(column_kernel, lev_count, row_count),
        out_shape=jax.ShapeDtypeStruct((feat, chunks * row_count, lon_count), jnp.bfloat16),
        in_specs=[pl.BlockSpec(memory_space=pl.ANY)] + [vmem] * 6,
        out_specs=vmem,
        scratch_shapes=[
            pltpu.VMEM((chunks, count, tall, width), jnp.bfloat16),
            pltpu.VMEM((tall, lon_count), jnp.float32),
            pltpu.VMEM((row_count, feat, lon_count), jnp.float32),
            pltpu.SemaphoreType.DMA((chunks, count)),
            pltpu.SemaphoreType.DMA((chunks, count)),
            pltpu.SemaphoreType.DMA((chunks,)),
        ],
        compiler_params=pltpu.CompilerParams(
            collective_id=1, has_side_effects=True, vmem_limit_bytes=vmem_limit
        ),
        name="back_and_columns",
    )(parcels, table, hot, norm_gain[:, None], w_first, w_mid, w_out)


def legendre_kernel(
    lev_count, land_ref, basis_ref, wave_ref, modes_ref, turned_ref, rates_ref, out_ref, back_ref,
    x_ref,
):
    count, layers, _, slots, lat_dev = land_ref.shape
    wide_count = count // lev_count
    _, fields, levels, _, wave_count = out_ref.shape
    lev_dev = layers // fields
    for w in range(wide_count):
        pieces = []
        for f in range(fields):
            for r in range(2):
                rows = jnp.concatenate(
                    [
                        land_ref[w * lev_count + l, f * lev_dev : (f + 1) * lev_dev, r]
                        for l in range(lev_count)
                    ],
                    axis=0,
                ).astype(jnp.float32)
                pieces.append(jnp.swapaxes(rows, 0, 1))
        x_ref[:, :, w * lat_dev : (w + 1) * lat_dev] = jnp.concatenate(pieces, axis=1).astype(
            jnp.bfloat16
        )
    position = lax.broadcasted_iota(jnp.int32, (1, wave_count), 1)

    def mixed(value, columns):
        total = columns[:, 0:1] * value[0:1, :]
        for l in range(1, levels):
            total = total + columns[:, l : l + 1] * value[l : l + 1, :]
        return total

    for s in range(slots):
        basis = basis_ref[s]
        raw = lax.dot_general(
            x_ref[s], basis, (((1,), (1,)), ((), ())), preferred_element_type=jnp.float32
        )
        wave = wave_ref[s : s + 1, 0:1]
        degree = wave + position
        raw = jnp.where(degree < wave_count, raw, 0.0)
        curvature = (degree * (degree + 1)).astype(jnp.float32) * (
            1.0 / float(wave_count * wave_count)
        )
        weight = jnp.where(wave == 0, 1.0, 2.0)
        parts = []
        for f in range(fields):
            scale = 1.0 / (1.0 + curvature * rates_ref[f])
            for r in range(2):
                first = (f * 2 + r) * levels
                value = raw[first : first + levels]
                if f == 0:
                    value = value * scale
                else:
                    value = mixed(mixed(value, turned_ref[...]) * scale, modes_ref[...])
                out_ref[s, f, :, r, :] = value
                parts.append(value)
        rounded = jnp.concatenate(parts, axis=0).astype(jnp.bfloat16)
        back = jnp.dot(rounded, basis, preferred_element_type=jnp.float32) * weight
        for r in range(2):
            back_ref[r, s] = jnp.concatenate(
                [
                    back[(f * 2 + r) * levels : (f * 2 + r + 1) * levels]
                    for f in range(fields)
                ],
                axis=0,
            ).astype(jnp.bfloat16)


def legendre(arrived, lat_basis, wave_part, vert_modes, vert_rates, lev_count, slots):
    slot_dev, wave_count, lat_count = lat_basis.shape
    count, layers, _, lat_dev = arrived.shape
    fields, levels = vert_rates.shape
    whole = lambda shape: pl.BlockSpec(shape, lambda i: (0,) * len(shape))
    return pl.pallas_call(
        functools.partial(legendre_kernel, lev_count),
        grid=(slot_dev // slots,),
        in_specs=[
            pl.BlockSpec((count, layers, 2, slots, lat_dev), lambda i: (0, 0, 0, i, 0)),
            pl.BlockSpec((slots, wave_count, lat_count), lambda i: (i, 0, 0)),
            pl.BlockSpec((slots, lane), lambda i: (i, 0)),
            whole((levels, levels)),
            whole((levels, levels)),
            whole((fields, levels, 1)),
        ],
        out_specs=[
            pl.BlockSpec((slots, fields, levels, 2, wave_count), lambda i: (i, 0, 0, 0, 0)),
            pl.BlockSpec((2, slots, fields * levels, lat_count), lambda i: (0, i, 0, 0)),
        ],
        out_shape=[
            jax.ShapeDtypeStruct((slot_dev, fields, levels, 2, wave_count), jnp.float32),
            jax.ShapeDtypeStruct((2, slot_dev, fields * levels, lat_count), jnp.bfloat16),
        ],
        scratch_shapes=[pltpu.VMEM((slots, 2 * fields * levels, lat_count), jnp.bfloat16)],
        compiler_params=pltpu.CompilerParams(vmem_limit_bytes=vmem_limit),
        name="legendre",
    )(
        arrived.reshape(count, layers, 2, slot_dev, lat_dev),
        lat_basis,
        jnp.broadcast_to(wave_part[:, None], (slot_dev, lane)),
        vert_modes,
        vert_modes.T,
        vert_rates[:, :, None],
    )


def legendre_plain(arrived, lat_basis, wave_part, vert_modes, vert_rates, wide_count, lev_count):
    slot_dev, wave_count, lat_count = lat_basis.shape
    _, layers, _, lat_dev = arrived.shape
    fields, levels = vert_rates.shape
    by_wave = arrived.reshape(
        wide_count, lev_count, fields, levels // lev_count, 2, slot_dev, lat_dev
    )
    by_wave = by_wave.transpose(5, 4, 2, 1, 3, 0, 6).reshape(
        slot_dev, 2, 1, fields, levels, lat_count
    )
    raw_spectra = jnp.einsum(
        "skj,srbflj->sbflrk", lat_basis, by_wave, preferred_element_type=jnp.float32
    )
    spectral = couple(raw_spectra, wave_part, vert_modes, vert_rates)
    weight = jnp.where(wave_part == 0, 1.0, 2.0).astype(jnp.bfloat16)
    back_coeffs = jnp.einsum(
        "skj,sbflrk->srbflj",
        lat_basis,
        spectral.astype(jnp.bfloat16),
        preferred_element_type=jnp.float32,
    ).astype(jnp.bfloat16)
    back_coeffs = back_coeffs * weight[:, None, None, None, None, None]
    back = back_coeffs.transpose(1, 0, 2, 3, 4, 5).reshape(
        2, slot_dev, fields * levels, lat_count
    )
    return (spectral[:, 0], back)


def band_rows(lat_first, lat_rows, band_sizes, band_bias, w_in):
    feat, bands = (w_in.shape[1], band_sizes.shape[0])
    band_ends = jnp.cumsum(band_sizes)
    band_starts = band_ends - band_sizes
    latitude = lat_first + jnp.arange(lat_rows, dtype=jnp.int32)
    inside = (
        (latitude[:, None] >= band_starts[None, :]) & (latitude[:, None] < band_ends[None, :])
    ).astype(jnp.float32)
    spare = -(feat + 2 * bands) % 16
    hot = jnp.pad(jnp.concatenate([inside, inside], axis=1), ((0, 0), (0, spare)))
    hot = jnp.broadcast_to(hot[:, :, None], hot.shape + (lane,))
    high = band_bias.astype(jnp.bfloat16)
    low = (band_bias - high.astype(jnp.float32)).astype(jnp.bfloat16)
    w_first = jnp.pad(jnp.concatenate([w_in, high, low], axis=1), ((0, 0), (0, spare)))
    return (hot, w_first * jnp.bfloat16(0.5))


def advect(grid_ref, before_ref, after_ref, adv_ref):
    fields, lev_dev, lat_dev, lon_count = grid_ref.shape
    blocks = lon_count // lane
    place = lax.broadcasted_iota(jnp.int32, (lat_dev, lane), 0)

    @pl.loop(0, lev_dev * blocks)
    def _(step):
        level = lax.rem(step, lev_dev)
        here = pl.ds(pl.multiple_of(step // lev_dev * lane, lane), lane)
        values = [grid_ref[f, level, :, here].astype(jnp.float32) for f in range(fields)]
        for f in range(fields):
            value = values[f]
            above = jnp.where(
                place == lat_dev - 1,
                after_ref[f, level, :, here].astype(jnp.float32),
                pltpu.roll(value, lat_dev - 1, 0),
            )
            below = jnp.where(
                place == 0,
                before_ref[f, level, :, here].astype(jnp.float32),
                pltpu.roll(value, 1, 0),
            )
            moved = transport_speed * values[(f + 1) % fields] * (above - below)
            adv_ref[f * lev_dev + level, :, here] = (value + moved).astype(jnp.bfloat16)


def fill_table(p_ref, q_ref, cos_ref, sin_ref, table_ref):
    rows = 256

    @pl.loop(0, table_ref.shape[0] // rows)
    def _(step):
        here = pl.ds(pl.multiple_of(step * rows, rows), rows)
        cos_b, sin_b = (cos_ref[here, :], sin_ref[here, :])
        p, q = (p_ref[here, :], q_ref[here, :])
        for a in range(p_ref.shape[1]):
            table_ref[here, a * lane : (a + 1) * lane] = (
                p[:, a : a + 1] * cos_b + q[:, a : a + 1] * sin_b
            ).astype(jnp.bfloat16)


def step_kernel(
    lev_count,
    grid_ref,
    before_ref,
    after_ref,
    p_ref,
    q_ref,
    cos_ref,
    sin_ref,
    basis_ref,
    wave_ref,
    modes_ref,
    turned_ref,
    rates_ref,
    hot_ref,
    gain_ref,
    w_first_ref,
    w_mid_ref,
    w_out_ref,
    spectral_ref,
    out_ref,
    held_grid,
    adv_ref,
    table_ref,
    send_one,
    land_one,
    basis_buf,
    x_ref,
    spectral_buf,
    back_ref,
    send_two,
    land_two,
    cell_ref,
    y_ref,
    send_sem,
    recv_sem,
    own_sem,
    basis_sem,
    spectral_sem,
    grid_sem,
):
    chunks, count, layers, tall, lat_dev = send_one.shape
    _, slots, wave_count, lat_count = basis_buf.shape
    fields, levels = spectral_buf.shape[2:4]
    lev_dev = layers // fields
    wide_count = count // lev_count
    feat = fields * levels
    lon_count = table_ref.shape[1]
    parts, row_count = (land_two.shape[0], land_two.shape[2] // feat)
    width = land_two.shape[3]
    lat_part = parts * row_count
    my_wide, my_lev = (lax.axis_index("wide"), lax.axis_index("lev"))
    me = my_wide * lev_count + my_lev

    fetch_grid = pltpu.make_async_copy(grid_ref, held_grid, grid_sem)
    fetch_grid.start()

    def fetch(c):
        here = pl.ds(pl.multiple_of(c * slots, slots), slots)
        part = lax.rem(c, 2)
        return pltpu.make_async_copy(
            basis_ref.at[here], basis_buf.at[part], basis_sem.at[part]
        )

    def store(c):
        here = pl.ds(pl.multiple_of(c * slots, slots), slots)
        part = lax.rem(c, 2)
        return pltpu.make_async_copy(
            spectral_buf.at[part], spectral_ref.at[here], spectral_sem.at[part]
        )

    def remote(which, source, target, c, k):
        return pltpu.make_async_remote_copy(
            src_ref=source,
            dst_ref=target,
            send_sem=send_sem.at[which, c, k],
            recv_sem=recv_sem.at[which, c, k],
            device_id=device_at(lax.rem(me + k, count), lev_count),
            device_id_type=mesh_id,
        )

    def first_out(c, k):
        peer = lax.rem(me + k, count)
        return remote(0, send_one.at[c, peer], land_one.at[c, me], c, k)

    def first_own(c):
        return pltpu.make_async_copy(
            send_one.at[c, me], land_one.at[c, me], own_sem.at[0, c]
        )

    def second_out(c, k):
        peer = lax.rem(me + k, count)
        return remote(1, send_two.at[peer, c], land_two.at[c, me], c, k)

    def second_own(c):
        return pltpu.make_async_copy(
            send_two.at[me, c], land_two.at[c, me], own_sem.at[1, c]
        )

    def send(out, own, c):
        @pl.loop(1, count)
        def _(k):
            out(c, k).start()

        own(c).start()

    def receive(out, own, c):
        own(c).wait()

        @pl.loop(1, count)
        def _(k):
            out(c, k).wait_recv()

    fetch(0).start()
    fetch(1).start()
    fill_table(p_ref, q_ref, cos_ref, sin_ref, table_ref)
    fetch_grid.wait()
    advect(held_grid, before_ref, after_ref, adv_ref)
    greet(me, count, lev_count)

    def transform(first, last):
        rows = (last - first) * tall

        @pl.loop(0, layers // 2)
        def _(g):
            wanted = jnp.concatenate(
                [
                    table_ref[q * width + first * tall : q * width + last * tall, :]
                    for q in range(count)
                ],
                axis=0,
            )
            pair = adv_ref[pl.ds(g * 2, 2)].reshape(2 * lat_dev, lon_count)
            result = lax.dot_general(
                wanted, pair, (((1,), (1,)), ((), ())), preferred_element_type=jnp.float32
            ).astype(jnp.bfloat16)
            for h in range(2):
                for q in range(count):
                    for c in range(first, last):
                        start = q * rows + (c - first) * tall
                        send_one[c, q, g * 2 + h] = result[
                            start : start + tall, h * lat_dev : (h + 1) * lat_dev
                        ]

    transform(0, 1)
    send(first_out, first_own, 0)
    transform(1, chunks)

    @pl.loop(1, chunks)
    def _(c):
        send(first_out, first_own, c)

    position = lax.broadcasted_iota(jnp.int32, (1, wave_count), 1)

    def mixed(value, columns):
        total = columns[:, 0:1] * value[0:1, :]
        for l in range(1, levels):
            total = total + columns[:, l : l + 1] * value[l : l + 1, :]
        return total

    @pl.loop(0, chunks)
    def _(c):
        part = lax.rem(c, 2)
        receive(first_out, first_own, c)
        for w in range(wide_count):
            pieces = []
            for f in range(fields):
                whole = jnp.concatenate(
                    [
                        land_one[c, w * lev_count + l, f * lev_dev : (f + 1) * lev_dev]
                        for l in range(lev_count)
                    ],
                    axis=0,
                ).astype(jnp.float32)
                for r in range(2):
                    pieces.append(jnp.swapaxes(whole[:, r * slots : (r + 1) * slots], 0, 1))
            x_ref[:, :, w * lat_dev : (w + 1) * lat_dev] = jnp.concatenate(
                pieces, axis=1
            ).astype(jnp.bfloat16)
        fetch(c).wait()

        @pl.when(c >= 2)
        def _():
            store(c - 2).wait()

        waves = wave_ref[pl.ds(pl.multiple_of(c * slots, slots), slots), :]
        for s in range(slots):
            basis = basis_buf[part, s]
            raw = lax.dot_general(
                x_ref[s], basis, (((1,), (1,)), ((), ())), preferred_element_type=jnp.float32
            )
            wave = waves[s : s + 1, 0:1]
            degree = wave + position
            raw = jnp.where(degree < wave_count, raw, 0.0)
            curvature = (degree * (degree + 1)).astype(jnp.float32) * (
                1.0 / float(wave_count * wave_count)
            )
            weight = jnp.where(wave == 0, 1.0, 2.0)
            parts_of = []
            for f in range(fields):
                scale = 1.0 / (1.0 + curvature * rates_ref[f])
                for r in range(2):
                    first = (f * 2 + r) * levels
                    value = raw[first : first + levels]
                    if f == 0:
                        value = value * scale
                    else:
                        value = mixed(mixed(value, turned_ref[...]) * scale, modes_ref[...])
                    spectral_buf[part, s, f, :, r, :] = value
                    parts_of.append(value)
            rounded = jnp.concatenate(parts_of, axis=0).astype(jnp.bfloat16)
            back = jnp.dot(rounded, basis, preferred_element_type=jnp.float32) * weight
            for r in range(2):
                columns = jnp.concatenate(
                    [
                        back[(f * 2 + r) * levels : (f * 2 + r + 1) * levels]
                        for f in range(fields)
                    ],
                    axis=0,
                )
                target = pl.ds(c * tall + (r * slots + s), feat, stride=width)
                for w in range(wide_count):
                    back_ref[w, target, :] = columns[:, w * lat_dev : (w + 1) * lat_dev]
        store(c).start()

        @pl.when(c + 2 < chunks)
        def _():
            fetch(c + 2).start()

    @pl.loop(0, wide_count)
    def _(i):
        w = lax.rem(my_wide + wide_count // 2 + i, wide_count)

        @pl.loop(0, feat // 2)
        def _(pair):
            turned = [
                back_ref[w, pl.ds(pl.multiple_of((pair * 2 + h) * width, width), width), :].T
                for h in range(2)
            ]
            here = pl.ds(pl.multiple_of(pair * 2 * row_count, 2 * row_count), 2 * row_count)
            for l in range(lev_count):
                for c in range(parts):
                    start = l * lat_part + c * row_count
                    send_two[w * lev_count + l, c, here, :] = jnp.concatenate(
                        [value[start : start + row_count] for value in turned], axis=0
                    ).astype(jnp.bfloat16)

        for l in range(lev_count):
            k = lax.rem(w * lev_count + l - me + count, count)

            @pl.when(k != 0)
            def _():
                second_out(0, k).start()

    second_own(0).start()

    @pl.loop(1, parts)
    def _(c):
        send(second_out, second_own, c)

    piece = lon_count // 2
    halves = lon_count // piece
    group = 4

    @pl.loop(0, parts)
    def _(c):
        receive(second_out, second_own, c)
        columns = jnp.concatenate([land_two[c, d] for d in range(count)], axis=1)
        cells = jnp.dot(columns, table_ref[...], preferred_element_type=jnp.float32)
        for b in range(lon_count // lane):
            cell_ref[b] = cells[:, b * lane : (b + 1) * lane]

        @pl.loop(0, row_count // group)
        def _(step_row):
            held = {}

            def place(unit):
                j = step_row * group + unit // halves
                start = unit % halves * piece
                return j, pl.ds(j, feat, stride=row_count), slice(start, start + piece)

            def enter(unit):
                j, rows, here = place(unit)
                hot = hot_ref[c * row_count + j]
                hot = jnp.concatenate([hot] * (piece // lane), axis=1)
                x = jnp.concatenate(
                    [
                        cell_ref[b, rows, :]
                        for b in range(here.start // lane, here.stop // lane)
                    ],
                    axis=1,
                )
                x = x.astype(jnp.bfloat16).astype(jnp.float32)
                average = jnp.sum(x * x, axis=0, keepdims=True) * (1.0 / feat)
                normed = x * lax.rsqrt(average + norm_eps) * gain_ref[...]
                entries = jnp.concatenate([normed, hot], axis=0).astype(jnp.bfloat16)
                half = jnp.dot(w_first_ref[...], entries, preferred_element_type=jnp.float32)
                held["x", unit] = x
                held["in", unit] = half.astype(jnp.bfloat16)

            def middle(unit):
                half = held.pop(("in", unit))
                first = half * jnp.tanh(half) + half
                half = jnp.dot(w_mid_ref[...], first, preferred_element_type=jnp.float32)
                held["mid", unit] = half.astype(jnp.bfloat16)

            def leave(unit):
                j, rows, here = place(unit)
                half = held.pop(("mid", unit))
                second = half * jnp.tanh(half) + half
                total = held.pop(("x", unit)) + jnp.dot(
                    w_out_ref[...], second, preferred_element_type=jnp.float32
                )
                for start in range(0, piece, lane):
                    y_ref[(here.start + start) // lane, rows, :] = total[:, start : start + lane]

            units = group * halves
            for step in range(units + 2):
                for late, stage in ((0, enter), (1, middle), (2, leave)):
                    if 0 <= step - late < units:
                        stage(step - late)

        finished = pl.ds(pl.multiple_of(c * row_count, row_count), row_count)
        for b in range(lon_count // lane):
            out_ref[:, finished, b * lane : (b + 1) * lane] = (
                y_ref[b].reshape(feat, row_count, lane).astype(jnp.bfloat16)
            )

    store(chunks - 2).wait()
    store(chunks - 1).wait()
    for out in (first_out, second_out):

        @pl.loop(0, chunks)
        def _(c):
            @pl.loop(1, count)
            def _(k):
                out(c, k).wait_send()


def fused_step(
    grid_state,
    before,
    after,
    wave_slots,
    wave_part,
    lat_basis,
    vert_modes,
    vert_rates,
    hot,
    norm_gain,
    w_first,
    w_mid,
    w_out,
    lev_count,
    count,
    slots,
    row_count,
):
    _, fields, lev_dev, lat_dev, lon_count = grid_state.shape
    slot_dev, wave_count, lat_count = lat_basis.shape
    levels = lev_dev * lev_count
    layers, feat = (fields * lev_dev, fields * levels)
    chunks, parts = (slot_dev // slots, lat_count // count // row_count)
    width, wide_count = (2 * slot_dev, count // lev_count)
    factors = phase_factors(wave_slots, count * chunks, lon_count)
    vmem = pl.BlockSpec(memory_space=pltpu.VMEM)
    anywhere = pl.BlockSpec(memory_space=pl.ANY)
    bf16, f32 = (jnp.bfloat16, jnp.float32)
    return pl.pallas_call(
        functools.partial(step_kernel, lev_count),
        out_shape=[
            jax.ShapeDtypeStruct((slot_dev, fields, levels, 2, wave_count), f32),
            jax.ShapeDtypeStruct((feat, parts * row_count, lon_count), bf16),
        ],
        in_specs=[anywhere] + [vmem] * 6 + [anywhere] + [vmem] * 9,
        out_specs=[anywhere, vmem],
        scratch_shapes=[
            pltpu.VMEM((fields, lev_dev, lat_dev, lon_count), bf16),
            pltpu.VMEM((layers, lat_dev, lon_count), bf16),
            pltpu.VMEM((count * width, lon_count), bf16),
            pltpu.VMEM((chunks, count, layers, 2 * slots, lat_dev), bf16),
            pltpu.VMEM((chunks, count, layers, 2 * slots, lat_dev), bf16),
            pltpu.VMEM((2, slots, wave_count, lat_count), bf16),
            pltpu.VMEM((slots, 2 * feat, lat_count), bf16),
            pltpu.VMEM((2, slots, fields, levels, 2, wave_count), f32),
            pltpu.VMEM((wide_count, feat * width, lat_dev), f32),
            pltpu.VMEM((count, parts, feat * row_count, width), bf16),
            pltpu.VMEM((parts, count, feat * row_count, width), bf16),
            pltpu.VMEM((lon_count // lane, feat * row_count, lane), f32),
            pltpu.VMEM((lon_count // lane, feat * row_count, lane), f32),
            pltpu.SemaphoreType.DMA((2, chunks, count)),
            pltpu.SemaphoreType.DMA((2, chunks, count)),
            pltpu.SemaphoreType.DMA((2, chunks)),
            pltpu.SemaphoreType.DMA((2,)),
            pltpu.SemaphoreType.DMA((2,)),
            pltpu.SemaphoreType.DMA,
        ],
        compiler_params=pltpu.CompilerParams(
            collective_id=2,
            has_side_effects=True,
            vmem_limit_bytes=vmem_limit,
        ),
        name="fused_step",
    )(
        grid_state[0],
        before[0],
        after[0],
        *factors,
        lat_basis,
        jnp.broadcast_to(wave_part[:, None], (slot_dev, lane)),
        vert_modes,
        vert_modes.T,
        vert_rates[:, :, None],
        hot,
        norm_gain[:, None],
        w_first,
        w_mid,
        w_out,
    )


def local(
    grid_state,
    wave_slots,
    lat_basis,
    vert_modes,
    vert_rates,
    band_sizes,
    norm_gain,
    w_in,
    band_bias,
    w_mid,
    w_out,
):
    members, fields, lev_dev, lat_dev, lon_count = grid_state.shape
    wide_count = lax.axis_size("wide")
    lev_count = lax.axis_size("lev")
    count = wide_count * lev_count
    slot_dev, wave_count, lat_count = lat_basis.shape
    levels = lev_dev * lev_count
    block_index = lax.axis_index("wide") * lev_count + lax.axis_index("lev")
    wave_part = lax.dynamic_slice_in_dim(wave_slots, block_index * slot_dev, slot_dev)

    before, after = edges(grid_state, "wide", 3)
    lat_part = lat_count // count
    feat = fields * levels
    row_count = 8 if lat_part % 8 == 0 else lat_part
    hot, w_first = band_rows(block_index * lat_part, lat_part, band_sizes, band_bias, w_in)
    half_mid = w_mid * jnp.bfloat16(0.5)
    slots = 8
    if (
        lat_dev == lane
        and 2 * slot_dev == lane
        and levels == slots
        and row_count == slots
        and lat_part * lev_count == lat_dev
        and lon_count % (2 * lane) == 0
        and members == 1
    ):
        spectral, new_state = fused_step(
            grid_state,
            before,
            after,
            wave_slots,
            wave_part,
            lat_basis,
            vert_modes,
            vert_rates,
            hot,
            norm_gain,
            w_first,
            half_mid,
            w_out,
            lev_count,
            count,
            slots,
            row_count,
        )
        return (
            spectral[:, None],
            new_state.reshape(members, fields, levels, lat_part, lon_count),
        )
    padded = jnp.concatenate([before, grid_state, after], axis=3)
    advected = advection_term(padded, grid_state)
    layers = members * fields * lev_dev
    coeffs, table = forward_dft(
        advected.reshape(layers, lat_dev, lon_count), wave_slots, count
    )
    arrived = exchange(coeffs, lev_count)
    if lat_dev % lane == 0 and slot_dev % slots == 0 and levels == slots:
        spectral, back = legendre(
            arrived, lat_basis, wave_part, vert_modes, vert_rates, lev_count, slots
        )
    else:
        spectral, back = legendre_plain(
            arrived, lat_basis, wave_part, vert_modes, vert_rates, wide_count, lev_count
        )
    spectral = spectral[:, None]
    turned = lax.optimization_barrier(
        back.reshape(2 * slot_dev, feat, lat_count)
    )
    parcels = turned.transpose(2, 1, 0).reshape(
        count, lat_part // row_count, row_count * feat, 2 * slot_dev
    )
    new_state = back_and_columns(
        parcels, table, hot, norm_gain, w_first, half_mid, w_out, lev_count, row_count
    ).reshape(members, fields, levels, lat_part, lon_count)
    return (spectral, new_state)


def solution(mesh):
    placed = (
        P(("groups", "fld"), None, "lev", "wide", None),
        P(),
        P(("wide", "lev"), None, None),
        P(),
        P(),
        P(),
        P(),
        P(),
        P(),
        P(),
        P(),
    )
    return jax.shard_map(
        local,
        mesh=mesh,
        in_specs=placed,
        out_specs=(
            P(("wide", "lev"), ("groups", "fld"), None, None, None, None),
            P(("groups", "fld"), None, None, ("wide", "lev"), None),
        ),
        check_vma=False,
    )
```
